32 devices in a mesh: dp: 16 (over z, x, core), tensor: 2 (over y).
Axes of the slice: x: 2, y: 2, z: 4, core: 2. Of those that a mesh axis runs over, the one named last changes fastest.
Arguments:
- block_input: bfloat16 [8192, 1024], P(('dp', 'tensor')), may hold values from -6 to 6
- cotangent: bfloat16 [8192, 1024], P(('dp', 'tensor')), may hold values from -6 to 6
- segment_ids: int32 [16, 512], P('dp'), may hold values from 0 to 2, never falling along the last dimension, each value on 1 to 384 neighbouring positions
- positions: int32 [16, 512], P('dp'), may hold values from 0 to 8191
- norm_gains: bfloat16 [2, 1024], P(None, 'dp'), may hold values from 0.25 to 1.75
- qk_gains: bfloat16 [2, 64], P(None, 'dp'), may hold values from 0.6 to 1.6
- w_query: bfloat16 [1024, 1024], P('dp', 'tensor'), may hold values from -0.1875 to 0.1875
- w_keyval: bfloat16 [2, 1024, 512], P(None, 'dp', 'tensor'), may hold values from -0.1875 to 0.1875
- w_output: bfloat16 [1024, 1024], P('tensor', 'dp'), may hold values from -0.75 to 0.75
- w_gate_up: bfloat16 [2, 1024, 4608], P(None, 'dp', 'tensor'), may hold values from -0.1875 to 0.1875
- w_down: bfloat16 [4608, 1024], P('tensor', 'dp'), may hold values from -0.09375 to 0.09375
Outputs:
- block_output: bfloat16 [8192, 1024], P(('dp', 'tensor'))
- grad_input: float32 [8192, 1024], P(('dp', 'tensor'))
- grad_norm_gains: float32 [2, 1024], P(None, 'dp')
- grad_qk_gains: float32 [2, 64], P(None, 'dp')
- grad_query: float32 [1024, 1024], P('dp', 'tensor')
- grad_keyval: float32 [2, 1024, 512], P(None, 'dp', 'tensor')
- grad_output: float32 [1024, 1024], P('tensor', 'dp')
- grad_gate_up: float32 [2, 1024, 4608], P(None, 'dp', 'tensor')
- grad_down: float32 [4608, 1024], P('tensor', 'dp')
The draws below stay inside these ranges and needn't reach their ends.
Inputs may be any that keep to these rules, and one draw needn't show every extreme that they name: `segment_ids`: ids never fall along a row; each document spans 1 to 384 tokens and one spans exactly that many.
All inputs are finite; a program needn't handle non-finite values.
Results may differ from the reference program's by a relative error of at most 0.028.
Values may be sent and summed in bfloat16 or wider, within the bound.
A program may use at most 128 MiB of HBM per device.

```python
import math
import jax
import jax.numpy as jnp
import numpy as np
from jax import lax

D = 1024
H = 16
KV = 8
HD = 64
FF = 4608
ROW_LEN = 512
ROWS = 16
TOKENS = 8192


def draw_qk_gains(key, part):
    values = jnp.exp(jax.random.uniform(key, (2, HD), jnp.float32, math.log(0.6), math.log(1.6)))
    return values.astype(jnp.bfloat16)


def touch_ends(array, rng, least, largest):
    longest = array.shape.index(max(array.shape))
    spots = []
    for shift in (0, 1):
        where = [jax.random.randint(jax.random.fold_in(rng, axis), (), 0, length) for axis, length in enumerate(array.shape)]
        where[longest] = (where[longest] + shift) % array.shape[longest]
        spots.append(tuple(where))
    return array.at[spots[0]].set(least).at[spots[1]].set(largest)


def raised(drawn, own_key, source, target, blocks, factor):
    def block_of(position):
        return (jnp.arange(drawn.shape[position]) // (drawn.shape[position] // blocks)).reshape((-1,) + (1,) * (drawn.ndim - 1 - position))

    one_side = jax.random.permutation(own_key, blocks)[block_of(target)]
    other_side = (block_of(target) + blocks // 2) % blocks
    return jnp.where((block_of(source) == one_side) | (block_of(source) == other_side), factor * drawn, drawn)


def block_levels(stream_key, dims, pieces, low, top_value):
    factor_of, own = 1.0, jax.random.fold_in(stream_key, 6)
    for position, parts in pieces:
        draws = jnp.exp(jax.random.uniform(jax.random.fold_in(own, position), (parts,), jnp.float32, low / len(pieces), top_value / len(pieces)))
        factor_of = factor_of * jnp.repeat(draws, dims[position] // parts).reshape([-1 if axis == position else 1 for axis in range(len(dims))])
    return factor_of


def split_up(amount, total, reach, slope):
    weights = [(1 << 20) // math.isqrt(standing ** slope) + 1 for standing in range(2, amount + 1)]
    surplus, counts = total - reach - (amount - 1), [1] * (amount - 1)
    while surplus > 0:
        movable = [i for i in range(amount - 1) if counts[i] < reach]
        pool, remaining = sum([weights[i] for i in movable]), surplus
        for i in movable:
            addition = min(reach - counts[i], max(1, remaining * weights[i] // pool), surplus)
            counts[i] = counts[i] + addition
            surplus = surplus - addition
    return np.array([reach] + counts)


def uneven_parts(own_key, number_of, total, bound, skew):
    if number_of == 2:
        one = jax.random.randint(own_key, (), max(1, total - bound), min(bound, total - 1) + 1)
        return jnp.stack([one, total - one])
    sizes = jnp.asarray(split_up(number_of, total, bound, skew), jnp.int32)
    couples = (number_of - 1) // 2
    giver, receiver = sizes[1:1 + 2 * couples:2], sizes[2:2 + 2 * couples:2]
    margin = jnp.minimum(giver - 1, bound - receiver)
    moved = jax.random.randint(jax.random.fold_in(own_key, 1), (couples,), 0, 1 << 20) % (margin + 1)
    sizes = sizes.at[1:1 + 2 * couples:2].set(giver - moved).at[2:2 + 2 * couples:2].set(receiver + moved)
    return sizes[jax.random.permutation(jax.random.fold_in(own_key, 2), number_of)]


def centred(own_key, shape, scale, most, shards=(), kind=jnp.bfloat16):
    result = jax.random.normal(own_key, shape, jnp.float32) * scale
    if len(shards) > 0:
        result = block_levels(own_key, shape, shards, -0.22, 0.18) * result
    return jnp.clip(result, min=-most, max=most).astype(kind)


def heavy_noise(stream_key, extent, spread, bound, shards, heavy, held_as=jnp.bfloat16):
    values = spread * jax.random.normal(stream_key, extent, jnp.float32)
    if shards:
        values = values * block_levels(stream_key, extent, shards, -0.22, 0.18)
    return jnp.clip(raised(values, jax.random.fold_in(stream_key, 3), *heavy), -bound, bound).astype(held_as)


def setup_inputs(seed: int = 0) -> dict:
    seeds = jax.random.split(jax.random.key(seed), 12)
    block_input = centred(seeds[0], (TOKENS, D), 1.0, 6.0, ((0, 32),))
    cotangent = heavy_noise(seeds[1], (TOKENS, D), 1.0, 6.0, ((0, 32),), (0, 1, 32, 2.75))
    segment_ids = jax.vmap(lambda own: jnp.searchsorted(jnp.cumsum(uneven_parts(own, 3, ROW_LEN, ROW_LEN * 3 // 4, 0)), jnp.arange(ROW_LEN), side="right"))(jax.random.split(seeds[2], ROWS)).reshape((ROWS, ROW_LEN)).astype(jnp.int32)
    positions = touch_ends(jax.random.randint(seeds[3], (ROWS, ROW_LEN), 0, 8192), jax.random.fold_in(seeds[3], 1), 0, 8191).astype(jnp.int32)
    norm_gains = jnp.clip(1.0 + 0.15 * jax.random.normal(seeds[4], (2, D), jnp.float32), 0.25, 1.75).astype(jnp.bfloat16)
    qk_gains = draw_qk_gains(jax.random.fold_in(seeds[11], 71), 0)
    w_query = centred(seeds[6], (D, H * HD), D ** -0.5, 0.1875, ((0, 16), (1, 2)))
    w_keyval = centred(seeds[7], (2, D, KV * HD), D ** -0.5, 0.1875, ((1, 16), (2, 2)))
    w_output = centred(seeds[8], (H * HD, D), (H * HD // 16) ** -0.5, 0.75, ((0, 2), (1, 16)))
    w_gate_up = centred(seeds[9], (2, D, FF), D ** -0.5, 0.1875, ((1, 16), (2, 2)))
    w_down = centred(seeds[10], (FF, D), FF ** -0.5, 0.09375, ((0, 2), (1, 16)))
    return dict(block_input=block_input, cotangent=cotangent, segment_ids=segment_ids, positions=positions, norm_gains=norm_gains, qk_gains=qk_gains, w_query=w_query, w_keyval=w_keyval, w_output=w_output, w_gate_up=w_gate_up, w_down=w_down)


EPSILON = 1e-05
ROPE_BASE = 1000000.0
NEG_FILL = -1e+30

def rms_forward(values, gain):
    scale = lax.rsqrt(lax.optimization_barrier(jnp.mean(values * values, axis=-1, keepdims=True)) + EPSILON)
    return (values * scale * gain, scale)

def rms_backward(values, scale, gain, grad):
    weighted = grad * gain
    inner = lax.optimization_barrier(jnp.mean(weighted * values, axis=-1, keepdims=True))
    return scale * (weighted - values * scale * scale * inner)

def rope_tables(places):
    freqs = ROPE_BASE ** (-jnp.arange(0, HD, 2).astype(jnp.float32) / HD)
    angles = places.astype(jnp.float32)[..., None] * freqs
    angles = jnp.concatenate([angles, angles], axis=-1)
    return (jnp.cos(angles), jnp.sin(angles))

def rotate_half(values):
    half = values.shape[-1] // 2
    return jnp.concatenate([-values[..., half:], values[..., :half]], axis=-1)

def rotate_back(values):
    half = values.shape[-1] // 2
    return jnp.concatenate([values[..., half:], -values[..., :half]], axis=-1)

def allowed_mask(segs):
    length = segs.shape[0]
    index = jnp.arange(length, dtype=jnp.int32)
    return (segs[:, None] == segs[None, :]) & (index[None, :] <= index[:, None])

def row_scores(q_rot, k_rot):
    kv_heads = k_rot.shape[1]
    groups = q_rot.shape[1] // kv_heads
    q_four = q_rot.reshape(q_rot.shape[0], kv_heads, groups, HD)
    scores = jnp.einsum('ikgd,jkd->kgij', q_four.astype(jnp.float32), k_rot.astype(jnp.float32))
    return (scores / math.sqrt(HD), q_four)

def attend_row(q_rot, k_rot, values, segs):
    scores, q_four = row_scores(q_rot, k_rot)
    allowed = allowed_mask(segs)[None, None]
    masked = jnp.where(allowed, scores, NEG_FILL)
    top = lax.optimization_barrier(jnp.max(masked, axis=-1, keepdims=True))
    expd = jnp.where(allowed, jnp.exp(masked - top), 0.0)
    total = lax.optimization_barrier(jnp.sum(expd, axis=-1, keepdims=True))
    probs = (expd / total).astype(jnp.bfloat16)
    log_total = top[..., 0] + jnp.log(total[..., 0])
    attended = jnp.einsum('kgij,jkd->ikgd', probs.astype(jnp.float32), values.astype(jnp.float32))
    return (attended.reshape(q_rot.shape).astype(jnp.bfloat16), log_total)

def back_row(q_rot, k_rot, values, grad_att, log_total, segs):
    scores, q_four = row_scores(q_rot, k_rot)
    allowed = allowed_mask(segs)[None, None]
    masked = jnp.where(allowed, scores, NEG_FILL)
    probs = jnp.where(allowed, jnp.exp(masked - log_total[..., None]), 0.0)
    probs_b = probs.astype(jnp.bfloat16)
    grad_four = grad_att.reshape(q_four.shape).astype(jnp.float32)
    grad_values = jnp.einsum('kgij,ikgd->jkd', probs_b.astype(jnp.float32), grad_four)
    grad_p = jnp.einsum('ikgd,jkd->kgij', grad_four, values.astype(jnp.float32))
    delta = lax.optimization_barrier(jnp.sum(probs * grad_p, axis=-1, keepdims=True))
    d_scores = (probs * (grad_p - delta) / math.sqrt(HD)).astype(jnp.bfloat16).astype(jnp.float32)
    grad_q = jnp.einsum('kgij,jkd->ikgd', d_scores, k_rot.astype(jnp.float32)).reshape(q_rot.shape)
    grad_k = jnp.einsum('kgij,ikgd->jkd', d_scores, q_four.astype(jnp.float32))
    return (grad_q, grad_k, grad_values)

def fdot(left, right):
    return jnp.dot(left, right, preferred_element_type=jnp.float32)

def run_block(x_blk, dy_blk, seg_blk, pos_blk, params):
    gain_attn, gain_ffn, gain_q, gain_k, w_q, w_k, w_v, w_o, w_g, w_u, w_d = params
    rows_n = seg_blk.shape[0]
    tokens_n = rows_n * ROW_LEN
    xfull = x_blk.astype(jnp.float32)
    normed_f, scale1 = rms_forward(xfull, gain_attn)
    normed1 = normed_f.astype(jnp.bfloat16)
    query = fdot(normed1, w_q).reshape(rows_n, ROW_LEN, H, HD)
    keys = fdot(normed1, w_k).reshape(rows_n, ROW_LEN, KV, HD)
    values = fdot(normed1, w_v).astype(jnp.bfloat16).reshape(rows_n, ROW_LEN, KV, HD)
    q_norm, q_scale = rms_forward(query, gain_q)
    k_norm, k_scale = rms_forward(keys, gain_k)
    cosv, sinv = rope_tables(pos_blk)
    cosv = cosv[:, :, None, :]
    sinv = sinv[:, :, None, :]
    q_rot = (q_norm * cosv + rotate_half(q_norm) * sinv).astype(jnp.bfloat16)
    k_rot = (k_norm * cosv + rotate_half(k_norm) * sinv).astype(jnp.bfloat16)
    attended, log_total = jax.vmap(attend_row)(q_rot, k_rot, values, seg_blk)
    att_flat = attended.reshape(tokens_n, H * HD)
    hidden = xfull + fdot(att_flat, w_o)
    normed_g, scale2 = rms_forward(hidden, gain_ffn)
    normed2 = normed_g.astype(jnp.bfloat16)
    gate_proj = fdot(normed2, w_g)
    up_proj = fdot(normed2, w_u)
    sigmoid_gate = jax.nn.sigmoid(gate_proj)
    silu_gate = gate_proj * sigmoid_gate
    act = (silu_gate * up_proj).astype(jnp.bfloat16)
    out_blk = (hidden + fdot(act, w_d)).astype(jnp.bfloat16)
    grad_act = fdot(dy_blk, w_d.T)
    grad_down = fdot(act.T, dy_blk)
    d_gate = (grad_act * up_proj * sigmoid_gate * (1.0 + gate_proj * (1.0 - sigmoid_gate))).astype(jnp.bfloat16)
    d_up = (grad_act * silu_gate).astype(jnp.bfloat16)
    grad_gate = fdot(normed2.T, d_gate)
    grad_up = fdot(normed2.T, d_up)
    grad_n2 = fdot(d_gate, w_g.T) + fdot(d_up, w_u.T)
    gain_ffn_grad = lax.optimization_barrier(jnp.sum(grad_n2 * hidden * scale2, axis=0))
    grad_hidden = dy_blk.astype(jnp.float32) + rms_backward(hidden, scale2, gain_ffn, grad_n2)
    grad_hidden_b = grad_hidden.astype(jnp.bfloat16)
    grad_att = fdot(grad_hidden_b, w_o.T).astype(jnp.bfloat16).reshape(rows_n, ROW_LEN, H, HD)
    grad_out = fdot(att_flat.T, grad_hidden_b)
    grad_qrot, grad_krot, grad_vals = jax.vmap(back_row)(q_rot, k_rot, values, grad_att, log_total, seg_blk)
    grad_qn = grad_qrot * cosv + rotate_back(grad_qrot * sinv)
    grad_kn = grad_krot * cosv + rotate_back(grad_krot * sinv)
    gain_q_grad = lax.optimization_barrier(jnp.sum(grad_qn * query * q_scale, axis=(0, 1, 2)))
    gain_k_grad = lax.optimization_barrier(jnp.sum(grad_kn * keys * k_scale, axis=(0, 1, 2)))
    d_query = rms_backward(query, q_scale, gain_q, grad_qn).astype(jnp.bfloat16).reshape(tokens_n, H * HD)
    d_keys = rms_backward(keys, k_scale, gain_k, grad_kn).astype(jnp.bfloat16).reshape(tokens_n, KV * HD)
    d_values = grad_vals.astype(jnp.bfloat16).reshape(tokens_n, KV * HD)
    grad_wq = fdot(normed1.T, d_query)
    grad_wk = fdot(normed1.T, d_keys)
    grad_wv = fdot(normed1.T, d_values)
    grad_n1 = fdot(d_query, w_q.T) + fdot(d_keys, w_k.T) + fdot(d_values, w_v.T)
    gain_attn_grad = lax.optimization_barrier(jnp.sum(grad_n1 * xfull * scale1, axis=0))
    grad_x = grad_hidden + rms_backward(xfull, scale1, gain_attn, grad_n1)
    grads = (gain_attn_grad, gain_ffn_grad, gain_q_grad, gain_k_grad, grad_wq, grad_wk, grad_wv, grad_out, grad_gate, grad_up, grad_down)
    return (out_blk, grad_x, grads)

def reference(block_input, cotangent, segment_ids, positions, norm_gains, qk_gains, w_query, w_keyval, w_output, w_gate_up, w_down):
    block_rows = math.gcd(ROWS, 8)
    blocks = ROWS // block_rows
    params = (norm_gains[0].astype(jnp.float32), norm_gains[1].astype(jnp.float32), qk_gains[0].astype(jnp.float32), qk_gains[1].astype(jnp.float32), w_query, w_keyval[0], w_keyval[1], w_output, w_gate_up[0], w_gate_up[1], w_down)
    inputs_b = block_input.reshape(blocks, block_rows * ROW_LEN, D)
    cotan_b = cotangent.reshape(blocks, block_rows * ROW_LEN, D)
    segs_b = segment_ids.reshape(blocks, block_rows, ROW_LEN)
    places_b = positions.reshape(blocks, block_rows, ROW_LEN)
    shapes = [(D,), (D,), (HD,), (HD,), (D, H * HD), (D, KV * HD), (D, KV * HD), (H * HD, D), (D, FF), (D, FF), (FF, D)]
    start = tuple((jnp.zeros(shape, jnp.float32) for shape in shapes))

    def advance(carry, items):
        x_blk, dy_blk, seg_blk, pos_blk = items
        out_blk, grad_x, grads = run_block(x_blk, dy_blk, seg_blk, pos_blk, params)
        return (tuple((total + term for total, term in zip(carry, grads))), (out_blk, grad_x))
    totals, (outputs, grads_x) = lax.scan(advance, start, (inputs_b, cotan_b, segs_b, places_b))
    grad_norm = jnp.stack([totals[0], totals[1]])
    grad_qk = jnp.stack([totals[2], totals[3]])
    grad_kv = jnp.stack([totals[5], totals[6]])
    grad_gu = jnp.stack([totals[8], totals[9]])
    return (outputs.reshape(TOKENS, D), grads_x.reshape(TOKENS, D), grad_norm, grad_qk, totals[4], grad_kv, totals[7], grad_gu, totals[10])
```

```python
import functools
import math

import jax
import jax.numpy as jnp
from jax import lax
from jax.experimental import pallas as pl
from jax.experimental.pallas import tpu as pltpu
from jax.sharding import PartitionSpec as P

HD = 64


EPSILON = 1e-05
ROPE_BASE = 1000000.0
NEG_FILL = -1e30


def rms_forward(values, gain):
    scale = lax.rsqrt(jnp.mean(values * values, axis=-1, keepdims=True) + EPSILON)
    return (values * scale * gain, scale)


def rms_backward(values, scale, gain, grad):
    weighted = grad * gain
    inner = jnp.mean(weighted * values, axis=-1, keepdims=True)
    return scale * (weighted - values * scale * scale * inner)


def rope_tables(places):
    freqs = ROPE_BASE ** (-jnp.arange(0, HD, 2).astype(jnp.float32) / HD)
    angles = places.astype(jnp.float32)[..., None] * freqs
    angles = jnp.concatenate([angles, angles], axis=-1)
    return (jnp.cos(angles), jnp.sin(angles))


def rotate_half(values):
    half = values.shape[-1] // 2
    return jnp.concatenate([-values[..., half:], values[..., :half]], axis=-1)


def rotate_back(values):
    half = values.shape[-1] // 2
    return jnp.concatenate([values[..., half:], -values[..., :half]], axis=-1)


def allowed_mask(segs):
    length = segs.shape[0]
    index = jnp.arange(length, dtype=jnp.int32)
    return (segs[:, None] == segs[None, :]) & (index[None, :] <= index[:, None])


def contract(left, right, left_dim, right_dim):
    return lax.dot_general(
        left, right, (((left_dim,), (right_dim,)), ((), ())), preferred_element_type=jnp.float32
    )


def fdot(left, right):
    return jnp.dot(left, right, preferred_element_type=jnp.float32)


def row_scores(q_rot, k_rot):
    kv_heads = k_rot.shape[1]
    groups = q_rot.shape[1] // kv_heads
    q_four = q_rot.reshape(q_rot.shape[0], kv_heads, groups, HD)
    scores = jnp.einsum("ikgd,jkd->kgij", q_four, k_rot, preferred_element_type=jnp.float32)
    return (scores / math.sqrt(HD), q_four)


def attend_row(q_rot, k_rot, values, segs):
    scores, q_four = row_scores(q_rot, k_rot)
    allowed = allowed_mask(segs)[None, None]
    masked = jnp.where(allowed, scores, NEG_FILL)
    top = jnp.max(masked, axis=-1, keepdims=True)
    expd = jnp.where(allowed, jnp.exp(masked - top), 0.0)
    total = jnp.sum(expd, axis=-1, keepdims=True)
    probs = (expd / total).astype(jnp.bfloat16)
    log_total = top[..., 0] + jnp.log(total[..., 0])
    attended = jnp.einsum("kgij,jkd->ikgd", probs, values, preferred_element_type=jnp.float32)
    return (attended.reshape(q_rot.shape).astype(jnp.bfloat16), log_total)


def back_row(q_rot, k_rot, values, grad_att, log_total, segs):
    scores, q_four = row_scores(q_rot, k_rot)
    allowed = allowed_mask(segs)[None, None]
    masked = jnp.where(allowed, scores, NEG_FILL)
    probs = jnp.where(allowed, jnp.exp(masked - log_total[..., None]), 0.0)
    probs_b = probs.astype(jnp.bfloat16)
    grad_four = grad_att.reshape(q_four.shape)
    grad_values = jnp.einsum(
        "kgij,ikgd->jkd", probs_b, grad_four, preferred_element_type=jnp.float32
    )
    grad_p = jnp.einsum("ikgd,jkd->kgij", grad_four, values, preferred_element_type=jnp.float32)
    delta = jnp.sum(probs * grad_p, axis=-1, keepdims=True)
    d_scores = (probs * (grad_p - delta) / math.sqrt(HD)).astype(jnp.bfloat16)
    grad_q = jnp.einsum(
        "kgij,jkd->ikgd", d_scores, k_rot, preferred_element_type=jnp.float32
    ).reshape(q_rot.shape)
    grad_k = jnp.einsum("kgij,ikgd->jkd", d_scores, q_four, preferred_element_type=jnp.float32)
    return (grad_q, grad_k, grad_values)


def layout_of(dp):
    if dp == 16:
        return (4, 4, 2)
    return (dp // 4, 2, dp // 2)


class Place:
    def __init__(self, dp):
        self.length, self.zs, self.xs = layout_of(dp)
        me = lax.axis_index("dp")
        self.z = lax.rem(me // self.zs, self.length)
        self.x = lax.rem(me // self.xs, 2)
        self.c = lax.rem(me, 2)

    def device(self, z, x, c):
        return z * self.zs + x * self.xs + c

    def greet(self):
        z, x, c = self.z, self.x, self.c
        barrier = pltpu.get_barrier_semaphore()

        def signal(target):
            pl.semaphore_signal(
                barrier, inc=1, device_id={"dp": target}, device_id_type=pl.DeviceIdType.MESH
            )

        signal(self.device(z, x, 1 - c))
        signal(self.device(z, 1 - x, c))
        pl.when(z > 0)(lambda: signal(self.device(z - 1, x, c)))
        pl.when(z < self.length - 1)(lambda: signal(self.device(z + 1, x, c)))
        ends = jnp.where(z > 0, 1, 0) + jnp.where(z < self.length - 1, 1, 0)
        pl.semaphore_wait(barrier, 2 + ends)


def remote(src, dst, send, recv, target):
    return pltpu.make_async_remote_copy(
        src_ref=src,
        dst_ref=dst,
        send_sem=send,
        recv_sem=recv,
        device_id={"dp": target},
        device_id_type=pl.DeviceIdType.MESH,
    )


def gather_kernel(dp, count, rows, *refs):
    ins, outs = refs[:count], refs[count : 2 * count]
    send, recv, local = refs[2 * count :]
    at = Place(dp)
    z, x, c, length = at.z, at.x, at.c, at.length
    below, above = at.device(z - 1, x, c), at.device(z + 1, x, c)
    beside, sibling = at.device(z, 1 - x, c), at.device(z, x, 1 - c)
    at.greet()
    own = at.device(z, x, c)

    def slab(k, o):
        return outs[k].at[pl.ds(pl.multiple_of(o * rows, rows), rows)]

    for k in range(count):
        pltpu.make_async_copy(ins[k], slab(k, own), local.at[k]).start()

    def move(k, oz, ox, way, target, first):
        o = at.device(oz, ox, c)
        src = ins[k] if first else slab(k, o)
        return remote(src, slab(k, o), send.at[k, oz * 2 + ox, way], recv.at[k, o], target)

    def arrived(k, o):
        remote(slab(k, o), slab(k, o), send.at[k, 0, 0], recv.at[k, o], sibling).wait_recv()

    def steps(act):
        for s in range(length):
            for sign in (1, -1) if s else (0,):
                oz = z - s * sign

                def event(oz=oz, s=s, sign=sign):
                    for k in range(count):
                        act(k, oz, s, sign)

                if s:
                    pl.when((oz >= 0) & (oz < length))(event)
                else:
                    event()
            if s:
                side(s - 1, act)
        side(length - 1, act)

    def side(s, act):
        for sign in (1, -1) if s else (0,):
            oz = z - s * sign

            def event(oz=oz):
                for k in range(count):
                    act(k, oz, None, 0)

            if s:
                pl.when((oz >= 0) & (oz < length))(event)
            else:
                event()

    def begin(k, oz, s, sign):
        if s is None:
            arrived(k, at.device(oz, 1 - x, c))
            move(k, oz, 1 - x, 3, sibling, False).start()
            return
        first = s == 0
        if not first:
            arrived(k, at.device(oz, x, c))
        if sign >= 0:
            pl.when(z < length - 1)(lambda: move(k, oz, x, 0, above, first).start())
        if sign <= 0:
            pl.when(z > 0)(lambda: move(k, oz, x, 1, below, first).start())
        move(k, oz, x, 2, beside, first).start()
        move(k, oz, x, 3, sibling, first).start()

    def finish(k, oz, s, sign):
        if s is None:
            move(k, oz, 1 - x, 3, sibling, False).wait_send()
            return
        first = s == 0
        if sign >= 0:
            pl.when(z < length - 1)(lambda: move(k, oz, x, 0, above, first).wait_send())
        if sign <= 0:
            pl.when(z > 0)(lambda: move(k, oz, x, 1, below, first).wait_send())
        move(k, oz, x, 2, beside, first).wait_send()
        move(k, oz, x, 3, sibling, first).wait_send()

    steps(begin)
    for oz in range(length):
        for ox in range(2):
            for k in range(count):
                arrived(k, at.device(oz, ox, 1 - c))
    steps(finish)
    for k in range(count):
        pltpu.make_async_copy(ins[k], slab(k, own), local.at[k]).wait()


def gather_rows(arrays, dp):
    count, rows = len(arrays), arrays[0].shape[0]
    return pl.pallas_call(
        functools.partial(gather_kernel, dp, count, rows),
        out_shape=[jax.ShapeDtypeStruct((dp * rows, a.shape[1]), a.dtype) for a in arrays],
        in_specs=[pl.BlockSpec(memory_space=pltpu.VMEM)] * count,
        out_specs=[pl.BlockSpec(memory_space=pl.ANY)] * count,
        scratch_shapes=[
            pltpu.SemaphoreType.DMA((count, dp // 2, 4)),
            pltpu.SemaphoreType.DMA((count, dp)),
            pltpu.SemaphoreType.DMA((count,)),
        ],
        compiler_params=pltpu.CompilerParams(collective_id=1, has_side_effects=True),
        name="gather_rows",
    )(*arrays)


def scatter_kernel(dp, count, rows, *refs):
    parts, outs = refs[:count], refs[count : 2 * count]
    mine, first, second, upward, downward = (
        refs[(2 + i) * count : (3 + i) * count] for i in range(5)
    )
    sent1, sent2, sent4, got1, got2, got_up, got_down, local = refs[7 * count :]
    at = Place(dp)
    z, x, c, length = at.z, at.x, at.c, at.length
    below, above = at.device(z - 1, x, c), at.device(z + 1, x, c)
    beside, sibling = at.device(z, 1 - x, c), at.device(z, x, 1 - c)
    at.greet()

    def slab(k, o):
        return parts[k].at[pl.ds(pl.multiple_of(o * rows, rows), rows)]

    def swap(k, t, ox):
        q = t * 2 + ox
        return remote(
            slab(k, at.device(t, ox, 1 - c)), first[k].at[q], sent1.at[k, q], got1.at[k, q], sibling
        )

    def keep(k, t, ox):
        q = t * 2 + ox
        return pltpu.make_async_copy(slab(k, at.device(t, ox, c)), mine[k].at[q], local.at[k, q])

    def cross(k, t):
        q = t * 2 + 1 - x
        return remote(first[k].at[q], second[k].at[t], sent2.at[k, t], got2.at[k, t], beside)

    def rise(k, t):
        return remote(second[k].at[t], upward[k].at[t], sent4.at[k, t], got_up.at[k, t], above)

    def fall(k, t):
        return remote(second[k].at[t], downward[k].at[t], sent4.at[k, t], got_down.at[k, t], below)

    def targets(act):
        for d in range(length - 1, -1, -1):
            for sign in (1, -1) if d else (0,):
                t = z + d * sign

                def event(t=t, sign=sign):
                    for k in range(count):
                        act(k, t, sign)

                if d:
                    pl.when((t >= 0) & (t < length))(event)
                else:
                    event()

    def wide(value):
        return value.astype(jnp.float32)

    def start(k, t, sign):
        for ox in (1 - x, x):
            swap(k, t, ox).start()
            keep(k, t, ox).start()

    def chip_sum(k, t, sign):
        for ox in (1 - x, x):
            q = t * 2 + ox
            keep(k, t, ox).wait()
            swap(k, t, ox).wait_recv()
            first[k][q] = (wide(first[k][q]) + wide(mine[k][q])).astype(jnp.bfloat16)
            if ox is not x:
                cross(k, t).start()

    def chain(k, t, sign):
        cross(k, t).wait_recv()
        if sign == 0:
            outs[k][...] = wide(second[k][t]) + wide(first[k][t * 2 + x])

            def add_up():
                rise(k, t).wait_recv()
                outs[k][...] += wide(upward[k][t])

            def add_down():
                fall(k, t).wait_recv()
                outs[k][...] += wide(downward[k][t])

            pl.when(z > 0)(add_up)
            pl.when(z < length - 1)(add_down)
            return
        base, move = (upward, rise) if sign > 0 else (downward, fall)
        inner = z > 0 if sign > 0 else z < length - 1

        def middle():
            move(k, t).wait_recv()
            second[k][t] = (
                wide(second[k][t]) + wide(first[k][t * 2 + x]) + wide(base[k][t])
            ).astype(jnp.bfloat16)

        def edge():
            second[k][t] = (wide(second[k][t]) + wide(first[k][t * 2 + x])).astype(jnp.bfloat16)

        pl.when(inner)(middle)
        pl.when(jnp.logical_not(inner))(edge)
        move(k, t).start()

    def finish(k, t, sign):
        swap(k, t, 0).wait_send()
        swap(k, t, 1).wait_send()
        cross(k, t).wait_send()
        if sign:
            (rise if sign > 0 else fall)(k, t).wait_send()

    targets(start)
    targets(chip_sum)
    targets(chain)
    targets(finish)


def scatter_rows(arrays, dp):
    count, rows = len(arrays), arrays[0].shape[0] // dp
    length = layout_of(dp)[0]
    slots = [dp // 2, dp // 2, length, length, length]
    return pl.pallas_call(
        functools.partial(scatter_kernel, dp, count, rows),
        out_shape=[jax.ShapeDtypeStruct((rows, a.shape[1]), jnp.float32) for a in arrays],
        in_specs=[pl.BlockSpec(memory_space=pl.ANY)] * count,
        out_specs=[pl.BlockSpec(memory_space=pltpu.VMEM)] * count,
        scratch_shapes=[
            pltpu.VMEM((n, rows, a.shape[1]), a.dtype) for n in slots for a in arrays
        ]
        + [
            pltpu.SemaphoreType.DMA((count, n))
            for n in (dp // 2, length, length, dp // 2, length, length, length, dp // 2)
        ],
        compiler_params=pltpu.CompilerParams(
            collective_id=2, has_side_effects=True, vmem_limit_bytes=60 * 1024 * 1024
        ),
        name="scatter_rows",
    )(*arrays)


def exchange(values):
    return lax.ppermute(values, "tensor", ((0, 1), (1, 0)))


def collect(values):
    if lax.axis_size("tensor") != 2:
        return lax.all_gather(values, "tensor", axis=0, tiled=True)
    other = exchange(values)
    low = lax.axis_index("tensor") == 0
    return jnp.concatenate([jnp.where(low, values, other), jnp.where(low, other, values)])


def spread(values):
    if lax.axis_size("tensor") != 2:
        return lax.psum_scatter(values, "tensor", scatter_dimension=0, tiled=True)
    half = values.shape[0] // 2
    low = lax.axis_index("tensor") == 0
    head, tail = values[:half], values[half:]
    other = exchange(jnp.where(low, tail, head).astype(jnp.bfloat16))
    return jnp.where(low, head, tail) + other.astype(jnp.float32)


def total(values):
    if lax.axis_size("tensor") != 2:
        return lax.psum(values, "tensor")
    return values + exchange(values)


def on_device(
    block_input,
    cotangent,
    segment_ids,
    positions,
    norm_gains,
    qk_gains,
    w_query,
    w_keyval,
    w_output,
    w_gate_up,
    w_down,
):
    dp = lax.axis_size("dp")
    rows_here, row_len = segment_ids.shape
    tokens_here = rows_here * row_len
    shard, q_wide = w_query.shape
    kv_wide, ff_wide = w_keyval.shape[2], w_gate_up.shape[2]
    qk_shard = qk_gains.shape[1]
    gains = jnp.concatenate(
        [norm_gains.T, jnp.pad(qk_gains.T, ((0, shard - qk_shard), (0, 0)))], axis=1
    )
    gains = jnp.pad(gains, ((0, 0), (0, 124)))
    attn_pack = jnp.concatenate([w_query, w_keyval[0], w_keyval[1], w_output.T, gains], axis=1)
    gate_up_pack = jnp.concatenate([w_gate_up[0], w_gate_up[1]], axis=1)
    attn_full, gate_up_full, down_full = gather_rows([attn_pack, gate_up_pack, w_down.T], dp)
    qkv_wide = q_wide + 2 * kv_wide
    qkv_full = attn_full[:, :qkv_wide]
    output_full = attn_full[:, qkv_wide : qkv_wide + q_wide]
    gain_cols = attn_full[:, qkv_wide + q_wide :].astype(jnp.float32)
    gain_attn, gain_ffn = gain_cols[:, 0], gain_cols[:, 1]
    qk_cols = gain_cols.reshape(dp, shard, 128)[:, :qk_shard, 2:4].reshape(dp * qk_shard, 2)
    gain_q, gain_k = qk_cols[:, 0], qk_cols[:, 1]
    heads_here = q_wide // HD
    kv_here = kv_wide // HD
    dy_rows = collect(cotangent)
    xlocal = block_input.astype(jnp.float32)
    normed_f, scale1 = rms_forward(xlocal, gain_attn)
    normed1 = collect(normed_f.astype(jnp.bfloat16))
    qkv = fdot(normed1, qkv_full)
    query = qkv[:, :q_wide].reshape(rows_here, row_len, heads_here, HD)
    keys = qkv[:, q_wide : q_wide + kv_wide].reshape(rows_here, row_len, kv_here, HD)
    values = (
        qkv[:, q_wide + kv_wide :].astype(jnp.bfloat16).reshape(rows_here, row_len, kv_here, HD)
    )
    q_norm, q_scale = rms_forward(query, gain_q)
    k_norm, k_scale = rms_forward(keys, gain_k)
    cosv, sinv = rope_tables(positions)
    cosv = cosv[:, :, None, :]
    sinv = sinv[:, :, None, :]
    q_rot = (q_norm * cosv + rotate_half(q_norm) * sinv).astype(jnp.bfloat16)
    k_rot = (k_norm * cosv + rotate_half(k_norm) * sinv).astype(jnp.bfloat16)
    attended, log_total = jax.vmap(attend_row)(q_rot, k_rot, values, segment_ids)
    att_flat = attended.reshape(tokens_here, heads_here * HD)
    hidden = xlocal + spread(contract(att_flat, output_full, 1, 1))
    normed_g, scale2 = rms_forward(hidden, gain_ffn)
    normed2 = collect(normed_g.astype(jnp.bfloat16))
    gate_up = fdot(normed2, gate_up_full)
    gate_proj, up_proj = gate_up[:, :ff_wide], gate_up[:, ff_wide:]
    sigmoid_gate = jax.nn.sigmoid(gate_proj)
    silu_gate = gate_proj * sigmoid_gate
    act = (silu_gate * up_proj).astype(jnp.bfloat16)
    block_output = (hidden + spread(contract(act, down_full, 1, 1))).astype(jnp.bfloat16)
    grad_act = fdot(dy_rows, down_full)
    grad_down = contract(dy_rows, act, 0, 0).astype(jnp.bfloat16)
    d_gate = grad_act * up_proj * sigmoid_gate * (1.0 + gate_proj * (1.0 - sigmoid_gate))
    d_gate_up = jnp.concatenate(
        [d_gate.astype(jnp.bfloat16), (grad_act * silu_gate).astype(jnp.bfloat16)], axis=1
    )
    grad_gate_up = contract(normed2, d_gate_up, 0, 0).astype(jnp.bfloat16)
    grad_n2 = spread(contract(d_gate_up, gate_up_full, 1, 1))
    gain_ffn_grad = jnp.sum(grad_n2 * hidden * scale2, axis=0)
    grad_hidden = cotangent.astype(jnp.float32) + rms_backward(hidden, scale2, gain_ffn, grad_n2)
    grad_rows = collect(grad_hidden.astype(jnp.bfloat16))
    grad_att = (
        fdot(grad_rows, output_full)
        .astype(jnp.bfloat16)
        .reshape(rows_here, row_len, heads_here, HD)
    )
    grad_out = contract(grad_rows, att_flat, 0, 0).astype(jnp.bfloat16)
    grad_qrot, grad_krot, grad_vals = jax.vmap(back_row)(
        q_rot, k_rot, values, grad_att, log_total, segment_ids
    )
    grad_qn = grad_qrot * cosv + rotate_back(grad_qrot * sinv)
    grad_kn = grad_krot * cosv + rotate_back(grad_krot * sinv)
    gain_q_grad = jnp.sum(grad_qn * query * q_scale, axis=(0, 1, 2))
    gain_k_grad = jnp.sum(grad_kn * keys * k_scale, axis=(0, 1, 2))
    d_query = rms_backward(query, q_scale, gain_q, grad_qn).astype(jnp.bfloat16)
    d_keys = rms_backward(keys, k_scale, gain_k, grad_kn).astype(jnp.bfloat16)
    d_qkv = jnp.concatenate(
        [
            d_query.reshape(tokens_here, q_wide),
            d_keys.reshape(tokens_here, kv_wide),
            grad_vals.astype(jnp.bfloat16).reshape(tokens_here, kv_wide),
        ],
        axis=1,
    )
    grad_qkv = contract(normed1, d_qkv, 0, 0).astype(jnp.bfloat16)
    grad_n1 = spread(contract(d_qkv, qkv_full, 1, 1))
    gain_attn_grad = jnp.sum(grad_n1 * xlocal * scale1, axis=0)
    grad_input = grad_hidden + rms_backward(xlocal, scale1, gain_attn, grad_n1)
    gain_terms = total(
        jnp.concatenate([gain_attn_grad, gain_ffn_grad, gain_q_grad, gain_k_grad])[None]
    )[0]
    wide = dp * shard
    norm_terms = gain_terms[: 2 * wide].reshape(2, wide).T
    qk_terms = gain_terms[2 * wide :].reshape(2, dp, qk_shard).transpose(1, 2, 0)
    qk_terms = jnp.pad(qk_terms, ((0, 0), (0, shard - qk_shard), (0, 0))).reshape(wide, 2)
    gain_pack = jnp.concatenate([norm_terms, qk_terms], axis=1).astype(jnp.bfloat16)
    gain_pack = jnp.pad(gain_pack, ((0, 0), (0, 124)))
    grad_attn = jnp.concatenate([grad_qkv, grad_out, gain_pack], axis=1)
    attn_sum, gate_up_sum, down_sum = scatter_rows([grad_attn, grad_gate_up, grad_down], dp)
    gain_sum = attn_sum[:, qkv_wide + q_wide :]
    return (
        block_output,
        grad_input,
        gain_sum[:, 0:2].T,
        gain_sum[:qk_shard, 2:4].T,
        attn_sum[:, :q_wide],
        jnp.stack([attn_sum[:, q_wide : q_wide + kv_wide], attn_sum[:, q_wide + kv_wide : qkv_wide]]),
        attn_sum[:, qkv_wide : qkv_wide + q_wide].T,
        jnp.stack([gate_up_sum[:, :ff_wide], gate_up_sum[:, ff_wide:]]),
        down_sum.T,
    )


def solution(mesh):
    return jax.shard_map(
        on_device,
        mesh=mesh,
        in_specs=(
            P(("dp", "tensor"), None),
            P(("dp", "tensor"), None),
            P("dp", None),
            P("dp", None),
            P(None, "dp"),
            P(None, "dp"),
            P("dp", "tensor"),
            P(None, "dp", "tensor"),
            P("tensor", "dp"),
            P(None, "dp", "tensor"),
            P("tensor", "dp"),
        ),
        out_specs=(
            P(("dp", "tensor"), None),
            P(("dp", "tensor"), None),
            P(None, "dp"),
            P(None, "dp"),
            P("dp", "tensor"),
            P(None, "dp", "tensor"),
            P("tensor", "dp"),
            P(None, "dp", "tensor"),
            P("tensor", "dp"),
        ),
        check_vma=False,
    )
```

```python
import functools
import math

import jax
import jax.numpy as jnp
from jax import lax
from jax.experimental import pallas as pl
from jax.experimental.pallas import tpu as pltpu
from jax.sharding import PartitionSpec as P

HD = 64


EPSILON = 1e-05
ROPE_BASE = 1000000.0
NEG_FILL = -1e30


def rms_forward(values, gain):
    scale = lax.rsqrt(jnp.mean(values * values, axis=-1, keepdims=True) + EPSILON)
    return (values * scale * gain, scale)


def rms_backward(values, scale, gain, grad):
    weighted = grad * gain
    inner = jnp.mean(weighted * values, axis=-1, keepdims=True)
    return scale * (weighted - values * scale * scale * inner)


def rope_tables(places):
    freqs = ROPE_BASE ** (-jnp.arange(0, HD, 2).astype(jnp.float32) / HD)
    angles = places.astype(jnp.float32)[..., None] * freqs
    angles = jnp.concatenate([angles, angles], axis=-1)
    return (jnp.cos(angles), jnp.sin(angles))


def rotate_half(values):
    half = values.shape[-1] // 2
    return jnp.concatenate([-values[..., half:], values[..., :half]], axis=-1)


def rotate_back(values):
    half = values.shape[-1] // 2
    return jnp.concatenate([values[..., half:], -values[..., :half]], axis=-1)


def allowed_mask(segs):
    length = segs.shape[0]
    index = jnp.arange(length, dtype=jnp.int32)
    return (segs[:, None] == segs[None, :]) & (index[None, :] <= index[:, None])


def contract(left, right, left_dim, right_dim):
    return lax.dot_general(
        left, right, (((left_dim,), (right_dim,)), ((), ())), preferred_element_type=jnp.float32
    )


def fdot(left, right):
    return jnp.dot(left, right, preferred_element_type=jnp.float32)


def row_scores(q_rot, k_rot):
    kv_heads = k_rot.shape[1]
    groups = q_rot.shape[1] // kv_heads
    q_four = q_rot.reshape(q_rot.shape[0], kv_heads, groups, HD)
    scores = jnp.einsum("ikgd,jkd->kgij", q_four, k_rot, preferred_element_type=jnp.float32)
    return (scores / math.sqrt(HD), q_four)


def attend_row(q_rot, k_rot, values, segs):
    scores, q_four = row_scores(q_rot, k_rot)
    allowed = allowed_mask(segs)[None, None]
    masked = jnp.where(allowed, scores, NEG_FILL)
    top = jnp.max(masked, axis=-1, keepdims=True)
    expd = jnp.where(allowed, jnp.exp(masked - top), 0.0)
    total = jnp.sum(expd, axis=-1, keepdims=True)
    probs = (expd / total).astype(jnp.bfloat16)
    log_total = top[..., 0] + jnp.log(total[..., 0])
    attended = jnp.einsum("kgij,jkd->ikgd", probs, values, preferred_element_type=jnp.float32)
    return (attended.reshape(q_rot.shape).astype(jnp.bfloat16), log_total)


def back_row(q_rot, k_rot, values, grad_att, log_total, segs):
    scores, q_four = row_scores(q_rot, k_rot)
    allowed = allowed_mask(segs)[None, None]
    masked = jnp.where(allowed, scores, NEG_FILL)
    probs = jnp.where(allowed, jnp.exp(masked - log_total[..., None]), 0.0)
    probs_b = probs.astype(jnp.bfloat16)
    grad_four = grad_att.reshape(q_four.shape)
    grad_values = jnp.einsum(
        "kgij,ikgd->jkd", probs_b, grad_four, preferred_element_type=jnp.float32
    )
    grad_p = jnp.einsum("ikgd,jkd->kgij", grad_four, values, preferred_element_type=jnp.float32)
    delta = jnp.sum(probs * grad_p, axis=-1, keepdims=True)
    d_scores = (probs * (grad_p - delta) / math.sqrt(HD)).astype(jnp.bfloat16)
    grad_q = jnp.einsum(
        "kgij,jkd->ikgd", d_scores, k_rot, preferred_element_type=jnp.float32
    ).reshape(q_rot.shape)
    grad_k = jnp.einsum("kgij,ikgd->jkd", d_scores, q_four, preferred_element_type=jnp.float32)
    return (grad_q, grad_k, grad_values)


def layout_of(dp):
    if dp == 16:
        return (4, 4, 2)
    return (dp // 4, 2, dp // 2)


class Place:
    def __init__(self, dp):
        self.length, self.zs, self.xs = layout_of(dp)
        me = lax.axis_index("dp")
        self.z = lax.rem(me // self.zs, self.length)
        self.x = lax.rem(me // self.xs, 2)
        self.c = lax.rem(me, 2)

    def device(self, z, x, c):
        return z * self.zs + x * self.xs + c

    def greet(self):
        z, x, c = self.z, self.x, self.c
        barrier = pltpu.get_barrier_semaphore()

        def signal(target):
            pl.semaphore_signal(
                barrier, inc=1, device_id={"dp": target}, device_id_type=pl.DeviceIdType.MESH
            )

        signal(self.device(z, x, 1 - c))
        signal(self.device(z, 1 - x, c))
        pl.when(z > 0)(lambda: signal(self.device(z - 1, x, c)))
        pl.when(z < self.length - 1)(lambda: signal(self.device(z + 1, x, c)))
        ends = jnp.where(z > 0, 1, 0) + jnp.where(z < self.length - 1, 1, 0)
        pl.semaphore_wait(barrier, 2 + ends)


def remote(src, dst, send, recv, target):
    return pltpu.make_async_remote_copy(
        src_ref=src,
        dst_ref=dst,
        send_sem=send,
        recv_sem=recv,
        device_id={"dp": target},
        device_id_type=pl.DeviceIdType.MESH,
    )


def gather_kernel(dp, count, rows, *refs):
    ins, outs = refs[:count], refs[count : 2 * count]
    send, recv, local = refs[2 * count :]
    at = Place(dp)
    z, x, c, length = at.z, at.x, at.c, at.length
    below, above = at.device(z - 1, x, c), at.device(z + 1, x, c)
    beside, sibling = at.device(z, 1 - x, c), at.device(z, x, 1 - c)
    at.greet()
    own = at.device(z, x, c)

    def slab(k, o):
        return outs[k].at[pl.ds(pl.multiple_of(o * rows, rows), rows)]

    for k in range(count):
        pltpu.make_async_copy(ins[k], slab(k, own), local.at[k]).start()

    def move(k, oz, ox, way, target, first):
        o = at.device(oz, ox, c)
        src = ins[k] if first else slab(k, o)
        return remote(src, slab(k, o), send.at[k, oz * 2 + ox, way], recv.at[k, o], target)

    def arrived(k, o):
        remote(slab(k, o), slab(k, o), send.at[k, 0, 0], recv.at[k, o], sibling).wait_recv()

    def steps(act):
        for s in range(length):
            for sign in (1, -1) if s else (0,):
                oz = z - s * sign

                def event(oz=oz, s=s, sign=sign):
                    for k in range(count):
                        act(k, oz, s, sign)

                if s:
                    pl.when((oz >= 0) & (oz < length))(event)
                else:
                    event()
            if s:
                side(s - 1, act, range(1, count))
            else:
                side(0, act, (0,))
        side(length - 1, act, range(1, count))

    def side(s, act, chosen):
        for sign in (1, -1) if s else (0,):
            oz = z - s * sign

            def event(oz=oz):
                for k in chosen:
                    act(k, oz, None, 0)

            if s:
                pl.when((oz >= 0) & (oz < length))(event)
            else:
                event()

    def begin(k, oz, s, sign):
        if k == 0 and s != 0:
            for ox in (1 - x,) if s is None else (x, 1 - x):
                arrived(k, at.device(oz, ox, c))
                if sign >= 0:
                    pl.when(z < length - 1)(lambda: move(k, oz, ox, 0, above, False).start())
                if sign <= 0:
                    pl.when(z > 0)(lambda: move(k, oz, ox, 1, below, False).start())
                move(k, oz, ox, 3, sibling, False).start()
            return
        if s is None:
            arrived(k, at.device(oz, 1 - x, c))
            move(k, oz, 1 - x, 3, sibling, False).start()
            return
        first = s == 0
        if not first:
            arrived(k, at.device(oz, x, c))
        if sign >= 0:
            pl.when(z < length - 1)(lambda: move(k, oz, x, 0, above, first).start())
        if sign <= 0:
            pl.when(z > 0)(lambda: move(k, oz, x, 1, below, first).start())
        move(k, oz, x, 2, beside, first).start()
        move(k, oz, x, 3, sibling, first).start()

    def finish(k, oz, s, sign):
        if k == 0 and s != 0:
            for ox in (1 - x,) if s is None else (x, 1 - x):
                if sign >= 0:
                    pl.when(z < length - 1)(lambda: move(k, oz, ox, 0, above, False).wait_send())
                if sign <= 0:
                    pl.when(z > 0)(lambda: move(k, oz, ox, 1, below, False).wait_send())
                move(k, oz, ox, 3, sibling, False).wait_send()
            return
        if s is None:
            move(k, oz, 1 - x, 3, sibling, False).wait_send()
            return
        first = s == 0
        if sign >= 0:
            pl.when(z < length - 1)(lambda: move(k, oz, x, 0, above, first).wait_send())
        if sign <= 0:
            pl.when(z > 0)(lambda: move(k, oz, x, 1, below, first).wait_send())
        move(k, oz, x, 2, beside, first).wait_send()
        move(k, oz, x, 3, sibling, first).wait_send()

    steps(begin)
    for oz in range(length):
        for ox in range(2):
            for k in range(count):
                arrived(k, at.device(oz, ox, 1 - c))
    steps(finish)
    for k in range(count):
        pltpu.make_async_copy(ins[k], slab(k, own), local.at[k]).wait()


def gather_rows(arrays, dp):
    count, rows = len(arrays), arrays[0].shape[0]
    return pl.pallas_call(
        functools.partial(gather_kernel, dp, count, rows),
        out_shape=[jax.ShapeDtypeStruct((dp * rows, a.shape[1]), a.dtype) for a in arrays],
        in_specs=[pl.BlockSpec(memory_space=pltpu.VMEM)] * count,
        out_specs=[pl.BlockSpec(memory_space=pl.ANY)] * count,
        scratch_shapes=[
            pltpu.SemaphoreType.DMA((count, dp // 2, 4)),
            pltpu.SemaphoreType.DMA((count, dp)),
            pltpu.SemaphoreType.DMA((count,)),
        ],
        compiler_params=pltpu.CompilerParams(collective_id=1, has_side_effects=True),
        name="gather_rows",
    )(*arrays)


def scatter_kernel(dp, count, rows, *refs):
    parts, outs = refs[:count], refs[count : 2 * count]
    mine, first, second, upward, downward = (
        refs[(2 + i) * count : (3 + i) * count] for i in range(5)
    )
    sent1, sent2, sent4, got1, got2, got_up, got_down, local = refs[7 * count :]
    at = Place(dp)
    z, x, c, length = at.z, at.x, at.c, at.length
    below, above = at.device(z - 1, x, c), at.device(z + 1, x, c)
    beside, sibling = at.device(z, 1 - x, c), at.device(z, x, 1 - c)
    at.greet()

    def slab(k, o):
        return parts[k].at[pl.ds(pl.multiple_of(o * rows, rows), rows)]

    def swap(k, t, ox):
        q = t * 2 + ox
        return remote(
            slab(k, at.device(t, ox, 1 - c)), first[k].at[q], sent1.at[k, q], got1.at[k, q], sibling
        )

    def keep(k, t, ox):
        q = t * 2 + ox
        return pltpu.make_async_copy(slab(k, at.device(t, ox, c)), mine[k].at[q], local.at[k, q])

    def cross(k, t):
        q = t * 2 + 1 - x
        return remote(first[k].at[q], second[k].at[t], sent2.at[k, t], got2.at[k, t], beside)

    def rise(k, t):
        return remote(second[k].at[t], upward[k].at[t], sent4.at[k, t], got_up.at[k, t], above)

    def fall(k, t):
        return remote(second[k].at[t], downward[k].at[t], sent4.at[k, t], got_down.at[k, t], below)

    def targets(act):
        for d in range(length - 1, -1, -1):
            for sign in (1, -1) if d else (0,):
                t = z + d * sign

                def event(t=t, sign=sign):
                    for k in range(count):
                        act(k, t, sign)

                if d:
                    pl.when((t >= 0) & (t < length))(event)
                else:
                    event()

    def wide(value):
        return value.astype(jnp.float32)

    def start(k, t, sign):
        for ox in (1 - x, x):
            swap(k, t, ox).start()
            keep(k, t, ox).start()

    def chip_sum(k, t, sign):
        for ox in (1 - x, x):
            q = t * 2 + ox
            keep(k, t, ox).wait()
            swap(k, t, ox).wait_recv()
            first[k][q] = (wide(first[k][q]) + wide(mine[k][q])).astype(jnp.bfloat16)
            if ox is not x:
                cross(k, t).start()

    def chain(k, t, sign):
        cross(k, t).wait_recv()
        if sign == 0:
            outs[k][...] = wide(second[k][t]) + wide(first[k][t * 2 + x])

            def add_up():
                rise(k, t).wait_recv()
                outs[k][...] += wide(upward[k][t])

            def add_down():
                fall(k, t).wait_recv()
                outs[k][...] += wide(downward[k][t])

            pl.when(z > 0)(add_up)
            pl.when(z < length - 1)(add_down)
            return
        base, move = (upward, rise) if sign > 0 else (downward, fall)
        inner = z > 0 if sign > 0 else z < length - 1

        def middle():
            move(k, t).wait_recv()
            second[k][t] = (
                wide(second[k][t]) + wide(first[k][t * 2 + x]) + wide(base[k][t])
            ).astype(jnp.bfloat16)

        def edge():
            second[k][t] = (wide(second[k][t]) + wide(first[k][t * 2 + x])).astype(jnp.bfloat16)

        pl.when(inner)(middle)
        pl.when(jnp.logical_not(inner))(edge)
        move(k, t).start()

    def finish(k, t, sign):
        swap(k, t, 0).wait_send()
        swap(k, t, 1).wait_send()
        cross(k, t).wait_send()
        if sign:
            (rise if sign > 0 else fall)(k, t).wait_send()

    targets(start)
    targets(chip_sum)
    targets(chain)
    targets(finish)


def scatter_rows(arrays, dp):
    count, rows = len(arrays), arrays[0].shape[0] // dp
    length = layout_of(dp)[0]
    slots = [dp // 2, dp // 2, length, length, length]
    return pl.pallas_call(
        functools.partial(scatter_kernel, dp, count, rows),
        out_shape=[jax.ShapeDtypeStruct((rows, a.shape[1]), jnp.float32) for a in arrays],
        in_specs=[pl.BlockSpec(memory_space=pl.ANY)] * count,
        out_specs=[pl.BlockSpec(memory_space=pltpu.VMEM)] * count,
        scratch_shapes=[
            pltpu.VMEM((n, rows, a.shape[1]), a.dtype) for n in slots for a in arrays
        ]
        + [
            pltpu.SemaphoreType.DMA((count, n))
            for n in (dp // 2, length, length, dp // 2, length, length, length, dp // 2)
        ],
        compiler_params=pltpu.CompilerParams(
            collective_id=2, has_side_effects=True, vmem_limit_bytes=60 * 1024 * 1024
        ),
        name="scatter_rows",
    )(*arrays)


def exchange(values):
    return lax.ppermute(values, "tensor", ((0, 1), (1, 0)))


def collect(values):
    if lax.axis_size("tensor") != 2:
        return lax.all_gather(values, "tensor", axis=0, tiled=True)
    other = exchange(values)
    low = lax.axis_index("tensor") == 0
    return jnp.concatenate([jnp.where(low, values, other), jnp.where(low, other, values)])


def spread(values):
    if lax.axis_size("tensor") != 2:
        return lax.psum_scatter(values, "tensor", scatter_dimension=0, tiled=True)
    half = values.shape[0] // 2
    low = lax.axis_index("tensor") == 0
    head, tail = values[:half], values[half:]
    other = exchange(jnp.where(low, tail, head).astype(jnp.bfloat16))
    return jnp.where(low, head, tail) + other.astype(jnp.float32)


def total(values):
    if lax.axis_size("tensor") != 2:
        return lax.psum(values, "tensor")
    return values + exchange(values)


def on_device(
    block_input,
    cotangent,
    segment_ids,
    positions,
    norm_gains,
    qk_gains,
    w_query,
    w_keyval,
    w_output,
    w_gate_up,
    w_down,
):
    dp = lax.axis_size("dp")
    rows_here, row_len = segment_ids.shape
    tokens_here = rows_here * row_len
    shard, q_wide = w_query.shape
    kv_wide, ff_wide = w_keyval.shape[2], w_gate_up.shape[2]
    qk_shard = qk_gains.shape[1]
    gains = jnp.concatenate(
        [norm_gains.T, jnp.pad(qk_gains.T, ((0, shard - qk_shard), (0, 0)))], axis=1
    )
    gains = jnp.pad(gains, ((0, 0), (0, 124)))
    attn_pack = jnp.concatenate([w_query, w_keyval[0], w_keyval[1], w_output.T, gains], axis=1)
    gate_up_pack = jnp.concatenate([w_gate_up[0], w_gate_up[1]], axis=1)
    attn_full, gate_up_full, down_full = gather_rows([attn_pack, gate_up_pack, w_down.T], dp)
    qkv_wide = q_wide + 2 * kv_wide
    qkv_full = attn_full[:, :qkv_wide]
    output_full = attn_full[:, qkv_wide : qkv_wide + q_wide]
    gain_cols = attn_full[:, qkv_wide + q_wide :].astype(jnp.float32)
    gain_attn, gain_ffn = gain_cols[:, 0], gain_cols[:, 1]
    qk_cols = gain_cols.reshape(dp, shard, 128)[:, :qk_shard, 2:4].reshape(dp * qk_shard, 2)
    gain_q, gain_k = qk_cols[:, 0], qk_cols[:, 1]
    heads_here = q_wide // HD
    kv_here = kv_wide // HD
    dy_rows = collect(cotangent)
    xlocal = block_input.astype(jnp.float32)
    normed_f, scale1 = rms_forward(xlocal, gain_attn)
    normed1 = collect(normed_f.astype(jnp.bfloat16))
    qkv = fdot(normed1, qkv_full)
    query = qkv[:, :q_wide].reshape(rows_here, row_len, heads_here, HD)
    keys = qkv[:, q_wide : q_wide + kv_wide].reshape(rows_here, row_len, kv_here, HD)
    values = (
        qkv[:, q_wide + kv_wide :].astype(jnp.bfloat16).reshape(rows_here, row_len, kv_here, HD)
    )
    q_norm, q_scale = rms_forward(query, gain_q)
    k_norm, k_scale = rms_forward(keys, gain_k)
    cosv, sinv = rope_tables(positions)
    cosv = cosv[:, :, None, :]
    sinv = sinv[:, :, None, :]
    q_rot = (q_norm * cosv + rotate_half(q_norm) * sinv).astype(jnp.bfloat16)
    k_rot = (k_norm * cosv + rotate_half(k_norm) * sinv).astype(jnp.bfloat16)
    attended, log_total = jax.vmap(attend_row)(q_rot, k_rot, values, segment_ids)
    att_flat = attended.reshape(tokens_here, heads_here * HD)
    hidden = xlocal + spread(contract(att_flat, output_full, 1, 1))
    normed_g, scale2 = rms_forward(hidden, gain_ffn)
    normed2 = collect(normed_g.astype(jnp.bfloat16))
    gate_up = fdot(normed2, gate_up_full)
    gate_proj, up_proj = gate_up[:, :ff_wide], gate_up[:, ff_wide:]
    sigmoid_gate = jax.nn.sigmoid(gate_proj)
    silu_gate = gate_proj * sigmoid_gate
    act = (silu_gate * up_proj).astype(jnp.bfloat16)
    block_output = (hidden + spread(contract(act, down_full, 1, 1))).astype(jnp.bfloat16)
    grad_act = fdot(dy_rows, down_full)
    grad_down = contract(dy_rows, act, 0, 0).astype(jnp.bfloat16)
    d_gate = grad_act * up_proj * sigmoid_gate * (1.0 + gate_proj * (1.0 - sigmoid_gate))
    d_gate_up = jnp.concatenate(
        [d_gate.astype(jnp.bfloat16), (grad_act * silu_gate).astype(jnp.bfloat16)], axis=1
    )
    grad_gate_up = contract(normed2, d_gate_up, 0, 0).astype(jnp.bfloat16)
    grad_n2 = spread(contract(d_gate_up, gate_up_full, 1, 1))
    gain_ffn_grad = jnp.sum(grad_n2 * hidden * scale2, axis=0)
    grad_hidden = cotangent.astype(jnp.float32) + rms_backward(hidden, scale2, gain_ffn, grad_n2)
    grad_rows = collect(grad_hidden.astype(jnp.bfloat16))
    grad_att = (
        fdot(grad_rows, output_full)
        .astype(jnp.bfloat16)
        .reshape(rows_here, row_len, heads_here, HD)
    )
    grad_out = contract(grad_rows, att_flat, 0, 0).astype(jnp.bfloat16)
    grad_qrot, grad_krot, grad_vals = jax.vmap(back_row)(
        q_rot, k_rot, values, grad_att, log_total, segment_ids
    )
    grad_qn = grad_qrot * cosv + rotate_back(grad_qrot * sinv)
    grad_kn = grad_krot * cosv + rotate_back(grad_krot * sinv)
    gain_q_grad = jnp.sum(grad_qn * query * q_scale, axis=(0, 1, 2))
    gain_k_grad = jnp.sum(grad_kn * keys * k_scale, axis=(0, 1, 2))
    d_query = rms_backward(query, q_scale, gain_q, grad_qn).astype(jnp.bfloat16)
    d_keys = rms_backward(keys, k_scale, gain_k, grad_kn).astype(jnp.bfloat16)
    d_qkv = jnp.concatenate(
        [
            d_query.reshape(tokens_here, q_wide),
            d_keys.reshape(tokens_here, kv_wide),
            grad_vals.astype(jnp.bfloat16).reshape(tokens_here, kv_wide),
        ],
        axis=1,
    )
    grad_qkv = contract(normed1, d_qkv, 0, 0).astype(jnp.bfloat16)
    grad_n1 = spread(contract(d_qkv, qkv_full, 1, 1))
    gain_attn_grad = jnp.sum(grad_n1 * xlocal * scale1, axis=0)
    grad_input = grad_hidden + rms_backward(xlocal, scale1, gain_attn, grad_n1)
    gain_terms = total(
        jnp.concatenate([gain_attn_grad, gain_ffn_grad, gain_q_grad, gain_k_grad])[None]
    )[0]
    wide = dp * shard
    norm_terms = gain_terms[: 2 * wide].reshape(2, wide).T
    qk_terms = gain_terms[2 * wide :].reshape(2, dp, qk_shard).transpose(1, 2, 0)
    qk_terms = jnp.pad(qk_terms, ((0, 0), (0, shard - qk_shard), (0, 0))).reshape(wide, 2)
    gain_pack = jnp.concatenate([norm_terms, qk_terms], axis=1).astype(jnp.bfloat16)
    gain_pack = jnp.pad(gain_pack, ((0, 0), (0, 124)))
    grad_attn = jnp.concatenate([grad_qkv, grad_out, gain_pack], axis=1)
    attn_sum, gate_up_sum, down_sum = scatter_rows([grad_attn, grad_gate_up, grad_down], dp)
    gain_sum = attn_sum[:, qkv_wide + q_wide :]
    return (
        block_output,
        grad_input,
        gain_sum[:, 0:2].T,
        gain_sum[:qk_shard, 2:4].T,
        attn_sum[:, :q_wide],
        jnp.stack([attn_sum[:, q_wide : q_wide + kv_wide], attn_sum[:, q_wide + kv_wide : qkv_wide]]),
        attn_sum[:, qkv_wide : qkv_wide + q_wide].T,
        jnp.stack([gate_up_sum[:, :ff_wide], gate_up_sum[:, ff_wide:]]),
        down_sum.T,
    )


def solution(mesh):
    return jax.shard_map(
        on_device,
        mesh=mesh,
        in_specs=(
            P(("dp", "tensor"), None),
            P(("dp", "tensor"), None),
            P("dp", None),
            P("dp", None),
            P(None, "dp"),
            P(None, "dp"),
            P("dp", "tensor"),
            P(None, "dp", "tensor"),
            P("tensor", "dp"),
            P(None, "dp", "tensor"),
            P("tensor", "dp"),
        ),
        out_specs=(
            P(("dp", "tensor"), None),
            P(("dp", "tensor"), None),
            P(None, "dp"),
            P(None, "dp"),
            P("dp", "tensor"),
            P(None, "dp", "tensor"),
            P("tensor", "dp"),
            P(None, "dp", "tensor"),
            P("tensor", "dp"),
        ),
        check_vma=False,
    )
```
